32 devices in a mesh: groups: 2 (over y), seq: 8 (over z, x), head: 2 (over core).
Axes of the slice: x: 2, y: 2, z: 4, core: 2. Of those that a mesh axis runs over, the one named last changes fastest.
Arguments:
- queries: bfloat16 [2048, 1024], P(('groups', 'seq'), 'head'), parts along dimension 0, may hold values from -6 to 6
- key_rows: bfloat16 [2048, 2, 1024], P(('groups', 'seq'), None, 'head'), parts along dimension 0, may hold values from -6 to 6
- value_rows: bfloat16 [2048, 2, 1024], P(('groups', 'seq'), None, 'head'), parts along dimension 0, may hold values from -6 to 6
- strengths: float32 [8, 2, 2048], P('head', None, ('groups', 'seq')), parts along dimension 2, may hold values from 0.2 to 2, as said below
- log_gate: float32 [8, 2048], P('head', ('groups', 'seq')), parts along dimension 1, may hold values from -1.2 to 0, as said below
- keep_flag: int32 [2048], P(('groups', 'seq')), parts along dimension 0, may hold values 0 or 1
- norm_gain: float32 [1024], P('head'), may hold values from 0.1 to 1.9
- out_weight: bfloat16 [1024, 2048], P('head'), may hold values from -0.1875 to 0.1875
Outputs:
- projected: bfloat16 [2048, 2048], P(('groups', 'seq', 'head')), parts along dimension 0
The draws below stay inside these ranges and needn't reach their ends.
There are 2 independent parts, one for each index of `groups`. The reference program is written for one: setup_inputs(seed, part) draws one part's arguments, and reference() takes and returns one part's arrays. A program takes and returns all parts, laid end to end along the dimension named above; an argument that names none is the same for every part. Nothing has to cross between parts.
Inputs may be any that keep to these rules, and one draw needn't show every extreme that they name: `strengths`: reflection strength of each head, key and token. `log_gate`: logarithm of each head's decay at each token.
All inputs are finite; a program needn't handle non-finite values. No bound on the sum of `keep_flag` on one device may be relied on, other than what follows from the above.
Results may differ from the reference program's by a relative error of at most 0.0049.
Values may be sent and summed in bfloat16 or wider, within the bound.
A program may use at most 64 MiB of HBM per device.

```python
import math
import jax
import jax.numpy as jnp
from jax import lax

D = 2048
H = 8
DK = 128
DV = 128
BLOCK = 64
TOK_DEV = 128
SEQ = 1024


def slow_heads(key):
    ranking = jax.random.permutation(jax.random.fold_in(key, 101), H)
    return ranking < H // 2


def draw_strengths(key, part):
    slow_mask = slow_heads(key)[:, None, None]
    spread = jax.random.uniform(jax.random.fold_in(key, 7), (H, 2, SEQ), jnp.float32)
    fast_side = 0.2 + 1.6 * spread
    slow_side = 2.0 - 0.001 * spread
    return jnp.where(slow_mask, slow_side, fast_side).astype(jnp.float32)


def draw_log_gate(key, part):
    slow_mask = slow_heads(key)[:, None]
    shard_count = SEQ // TOK_DEV
    compute_speed = jnp.exp(jax.random.uniform(jax.random.fold_in(key, 11), (H, shard_count), jnp.float32, 0.0, math.log(4.0)))
    compute_speed = jnp.repeat(compute_speed, TOK_DEV, axis=1)
    items_per_second = jnp.exp(jax.random.uniform(jax.random.fold_in(key, 12), (H, SEQ), jnp.float32, math.log(0.5), 0.0))
    reference_speed = jnp.where(slow_mask, 0.15 / SEQ, 1.0 / 40.0)
    assignment_cells = jax.random.randint(jax.random.fold_in(key, 13), (2,), 0, SEQ)
    network_level_count = jax.random.uniform(jax.random.fold_in(key, 14), (2,), jnp.float32, 0.2, 0.4)
    sequence_indices = jnp.arange(SEQ)
    contiguous_span = jnp.sum(jnp.where(sequence_indices[None, :] == assignment_cells[:, None], jnp.log(1.0 - network_level_count)[:, None], 0.0), axis=0)
    return (-reference_speed * compute_speed * items_per_second + contiguous_span[None, :]).astype(jnp.float32)


def place_ends(values, rng, low, top_value):
    shape = values.shape
    index_at = [jax.random.randint(jax.random.fold_in(rng, axis), (), 0, shape[axis]) for axis in range(len(shape))]
    values = values.at[tuple(index_at)].set(low)
    longest = shape.index(max(shape))
    index_at[longest] = (index_at[longest] + 1) % shape[longest]
    return values.at[tuple(index_at)].set(top_value)


def block_levels(stream_key, extent, split, low, largest):
    def one(axis_at, parts):
        draws = jax.random.uniform(jax.random.fold_in(jax.random.fold_in(stream_key, 6), axis_at), (parts,), jnp.float32, low / len(split), largest / len(split))
        return jnp.repeat(jnp.exp(draws), extent[axis_at] // parts).reshape((-1,) + (1,) * (len(extent) - axis_at - 1))

    factor_of = one(*split[0])
    for cut in split[1:]:
        factor_of = factor_of * one(*cut)
    return factor_of


def normal_values(key, shape, deviation, limit, shards=(), kind=jnp.bfloat16):
    drawn = deviation * jax.random.normal(key, shape, jnp.float32)
    if shards:
        drawn = drawn * block_levels(key, shape, shards, -0.22, 0.18)
    return jnp.clip(drawn, -limit, limit).astype(kind)


def setup_inputs(seed: int = 0, part: int = 0) -> dict:
    key_of = jax.random.split(jax.random.key(seed), 9)
    part_keys = jax.random.split(jax.random.fold_in(key_of[8], part), 9)
    return {
        "queries": normal_values(part_keys[0], (SEQ, H * DK), 1.0, 6.0, ((0, 8), (1, 2))),
        "key_rows": normal_values(part_keys[1], (SEQ, 2, H * DK), 1.0, 6.0, ((0, 8), (2, 2))),
        "value_rows": normal_values(part_keys[2], (SEQ, 2, H * DV), 1.0, 6.0, ((0, 8), (2, 2))),
        "strengths": draw_strengths(jax.random.fold_in(jax.random.fold_in(key_of[8], part), 71), part),
        "log_gate": draw_log_gate(jax.random.fold_in(jax.random.fold_in(key_of[8], part), 71), part),
        "keep_flag": place_ends((jax.random.randint(part_keys[5], (SEQ,), 0, 4) < 3).astype(jnp.int32), jax.random.fold_in(part_keys[5], 1), 0, 1),
        "norm_gain": jnp.clip(1.0 + 0.18 * jax.random.normal(key_of[6], (H * DV,), jnp.float32), 0.1, 1.9),
        "out_weight": normal_values(key_of[7], (H * DV, D), (H * DV) ** -0.5, 0.1875, ((0, 2),)),
    }


def unit_rows(values_in):
    return values_in * lax.rsqrt(lax.optimization_barrier(jnp.sum(values_in * values_in, axis=-1, keepdims=True)) + 1e-06)

def block_pieces(q_unit, k_unit, v_rows, beta_eff, step_log):
    highest = lax.Precision.HIGHEST
    size = k_unit.shape[-2]
    query_count = q_unit.shape[-2]
    cum_log = jnp.cumsum(step_log, axis=-1)
    sequence_indices = jnp.arange(size)
    strict_lower = sequence_indices[:, None] > sequence_indices[None, :]
    lower_incl = sequence_indices[:, None] >= sequence_indices[None, :]
    log_gap = cum_log[..., :, None] - cum_log[..., None, :]
    decay_pair = jnp.where(lower_incl, jnp.exp(jnp.where(lower_incl, log_gap, 0.0)), 0.0)
    key_gram = jnp.einsum('...id,...jd->...ij', k_unit, k_unit, precision=highest)
    lower_part = jnp.where(strict_lower, beta_eff[..., :, None] * decay_pair * key_gram, 0.0)
    system = lower_part + jnp.eye(size, dtype=k_unit.dtype)
    wide_w = jax.scipy.linalg.solve_triangular(system, (beta_eff * jnp.exp(cum_log))[..., None] * k_unit, lower=True, unit_diagonal=True)
    wide_u = jax.scipy.linalg.solve_triangular(system, beta_eff[..., None] * v_rows, lower=True, unit_diagonal=True)
    last_log = cum_log[..., -1:]
    to_end = jnp.exp(last_log - cum_log)
    faded_keys = k_unit * to_end[..., None]
    eye_keys = jnp.eye(k_unit.shape[-1], dtype=k_unit.dtype)
    block_trans = jnp.exp(last_log)[..., None] * eye_keys - jnp.einsum('...ld,...le->...de', faded_keys, wide_w, precision=highest)
    block_bias = jnp.einsum('...ld,...le->...de', faded_keys, wide_u, precision=highest)
    query_log = cum_log[..., 1::2]
    query_pos = 2 * jnp.arange(query_count) + 1
    visible = query_pos[:, None] >= sequence_indices[None, :]
    query_gap = query_log[..., :, None] - cum_log[..., None, :]
    query_decay = jnp.where(visible, jnp.exp(jnp.where(visible, query_gap, 0.0)), 0.0)
    query_mix = query_decay * jnp.einsum('...td,...ld->...tl', q_unit, k_unit, precision=highest)
    local_out = jnp.einsum('...tl,...le->...te', query_mix, wide_u, precision=highest)
    reach_query = jnp.exp(query_log)[..., None] * q_unit - jnp.einsum('...tl,...ld->...td', query_mix, wide_w, precision=highest)
    return (local_out, reach_query, block_trans, block_bias)

def reference(queries, key_rows, value_rows, strengths, log_gate, keep_flag, norm_gain, out_weight):
    highest = lax.Precision.HIGHEST
    seq_len = queries.shape[0]
    head_count = strengths.shape[0]
    blocks = seq_len // BLOCK
    q_unit = unit_rows(queries.astype(jnp.float32).reshape(seq_len, head_count, DK))
    q_unit = q_unit.transpose(1, 0, 2).reshape(head_count, blocks, BLOCK, DK)
    k_unit = unit_rows(key_rows.astype(jnp.float32).reshape(seq_len, 2, head_count, DK))
    k_unit = k_unit.transpose(2, 0, 1, 3).reshape(head_count, blocks, 2 * BLOCK, DK)
    v_rows = value_rows.astype(jnp.float32).reshape(seq_len, 2, head_count, DV)
    v_rows = v_rows.transpose(2, 0, 1, 3).reshape(head_count, blocks, 2 * BLOCK, DV)
    live_flag = keep_flag.astype(jnp.float32)
    beta_eff = (strengths * live_flag[None, None, :]).transpose(0, 2, 1).reshape(head_count, blocks, 2 * BLOCK)
    first_log = log_gate * live_flag[None, :]
    step_log = jnp.stack([first_log, jnp.zeros_like(first_log)], axis=-1).reshape(head_count, blocks, 2 * BLOCK)

    def advance(state_now, pieces):
        q_block, k_block, v_block, b_block, g_block = pieces
        local_out, reach_query, block_trans, block_bias = block_pieces(q_block, k_block, v_block, b_block, g_block)
        out_rows = local_out + jnp.einsum('htd,hde->hte', reach_query, state_now, precision=highest)
        state_next = jnp.einsum('hde,hef->hdf', block_trans, state_now, precision=highest) + block_bias
        return (state_next, out_rows)
    start_state = jnp.zeros((head_count, DK, DV), jnp.float32)
    inputs_by_block = (q_unit.swapaxes(0, 1), k_unit.swapaxes(0, 1), v_rows.swapaxes(0, 1), beta_eff.swapaxes(0, 1), step_log.swapaxes(0, 1))
    _, block_outs = lax.scan(advance, start_state, inputs_by_block)
    attended = block_outs.transpose(0, 2, 1, 3).reshape(seq_len, head_count, DV)
    inv_rms = lax.rsqrt(lax.optimization_barrier(jnp.mean(attended * attended, axis=-1, keepdims=True)) + 1e-05)
    normed = (attended * inv_rms * norm_gain.reshape(head_count, DV)[None, :, :]).reshape(seq_len, head_count * DV).astype(jnp.bfloat16)
    return jnp.dot(normed.astype(jnp.float32), out_weight.astype(jnp.float32), preferred_element_type=jnp.float32).astype(jnp.bfloat16)
```

```python
import functools

import jax
import jax.numpy as jnp
from jax import lax
from jax.experimental import pallas as pl
from jax.experimental.pallas import tpu as pltpu
from jax.sharding import PartitionSpec as P

DK = 128
DV = 128
F32 = jnp.float32
BF16 = jnp.bfloat16


def swapped(value, axis, bit):
    return lax.ppermute(value, axis, [(i, i ^ 1 << bit) for i in range(lax.axis_size(axis))])


def split2(x):
    hi = x.astype(BF16)
    return hi, (x - hi.astype(F32)).astype(BF16)


def dot1(a, b):
    return jnp.dot(a, b, preferred_element_type=F32)


def mm3(a, b):
    return dot1(a[0], b[0]) + (dot1(a[0], b[1]) + dot1(a[1], b[0]))


def dot_nt(a, b):
    return lax.dot_general(a, b, (((1,), (1,)), ((), ())), preferred_element_type=F32)


def local_kernel(heads, q_ref, k_ref, v_ref, small_ref, maps_ref, reads_ref, a_sc, xh_sc, xl_sc):
    tok = q_ref.shape[0]
    size = 2 * tok
    width = heads * DK
    row_t = lax.broadcasted_iota(jnp.int32, (tok, tok), 0)
    col_t = lax.broadcasted_iota(jnp.int32, (tok, tok), 1)
    incl = row_t >= col_t
    strict = row_t > col_t
    small = small_ref[...]
    s1 = small.astype(BF16)
    rest = small - s1.astype(F32)
    s2 = rest.astype(BF16)
    s3 = (rest - s2.astype(F32)).astype(BF16)
    upper = jnp.where(row_t <= col_t, 1.0, 0.0).astype(BF16)
    cum = dot1(s1, upper) + (dot1(s2, upper) + dot1(s3, upper))
    srows = small.shape[0]
    cols = jnp.concatenate([small, cum, jnp.zeros((tok - 2 * srows, tok), F32)], axis=0).T

    row_i = lax.broadcasted_iota(jnp.int32, (size, size), 0)
    col_i = lax.broadcasted_iota(jnp.int32, (size, size), 1)
    time_r = jnp.where(row_i < tok, 2 * row_i, 2 * row_i - 2 * tok + 1)
    time_c = jnp.where(col_i < tok, 2 * col_i, 2 * col_i - 2 * tok + 1)

    for h in range(heads):
        kk = [k_ref[:, j * width + h * DK : j * width + (h + 1) * DK] for j in range(2)]
        keys = jnp.concatenate(kk, axis=0)
        gram = dot_nt(keys, keys)
        cum_col = cols[:, srows + 2 * heads + h : srows + 2 * heads + h + 1]
        cum_row = cum[2 * heads + h : 2 * heads + h + 1, :]
        decay = jnp.where(incl, jnp.exp(jnp.where(incl, cum_col - cum_row, 0.0)), 0.0)
        decay_s = jnp.where(strict, decay, 0.0)
        kf = keys.astype(F32)
        r2 = 1.0 / (jnp.sum(kf * kf, axis=-1, keepdims=True) + 1e-06)
        beta = jnp.concatenate([cols[:, h : h + 1], cols[:, heads + h : heads + h + 1]], axis=0)
        factor = jnp.concatenate(
            [jnp.concatenate([decay_s, decay_s], axis=1), jnp.concatenate([decay, decay_s], axis=1)], axis=0
        )
        a_full = (beta * r2) * factor * gram
        a_sc[h] = a_full
        first = jnp.where((time_r ^ time_c) == 1, a_full, 0.0)
        x0 = jnp.where(time_r == time_c, 1.0, 0.0) - first
        xh_sc[h], xl_sc[h] = split2(x0)

    bit = 1
    while 2 << bit <= size:
        low = time_c >> bit
        picked = ((time_r >> bit) == (low | 1)) & ((low & 1) == 0)
        for h in range(heads):
            b = split2(jnp.where(picked, a_sc[h], 0.0))
            x = (xh_sc[h], xl_sc[h])
            y = split2(mm3(b, x))
            d = split2(mm3(x, y))
            xh_sc[h] = x[0] - d[0]
            xl_sc[h] = x[1] - d[1]
        bit += 1

    for h in range(heads):
        kk = [k_ref[:, j * width + h * DK : j * width + (h + 1) * DK] for j in range(2)]
        vv = [v_ref[:, j * width + h * DV : j * width + (h + 1) * DV] for j in range(2)]
        keys = jnp.concatenate(kk, axis=0)
        vals = jnp.concatenate(vv, axis=0).astype(F32)
        kf = keys.astype(F32)
        ss = jnp.sum(kf * kf, axis=-1, keepdims=True) + 1e-06
        beta = jnp.concatenate([cols[:, h : h + 1], cols[:, heads + h : heads + h + 1]], axis=0)
        cum_col = cols[:, srows + 2 * heads + h : srows + 2 * heads + h + 1]
        cum_row = cum[2 * heads + h : 2 * heads + h + 1, :]
        ecum = jnp.exp(cum_col)
        ecum2 = jnp.concatenate([ecum, ecum], axis=0)
        rhs = jnp.concatenate([(beta * ecum2 / ss) * kf, (beta * lax.rsqrt(ss)) * vals], axis=1)
        wu = mm3((xh_sc[h], xl_sc[h]), split2(rhs))
        q = q_ref[:, h * DK : (h + 1) * DK]
        qf = q.astype(F32)
        rq = lax.rsqrt(jnp.sum(qf * qf, axis=-1, keepdims=True) + 1e-06)
        decay = jnp.where(incl, jnp.exp(jnp.where(incl, cum_col - cum_row, 0.0)), 0.0)
        qmix = jnp.concatenate([decay, decay], axis=1) * (rq * dot_nt(q, keys))
        last = cum_row[:, tok - 1 : tok]
        to_end = jnp.exp(last - cum_row)
        kt = kf.T * jnp.concatenate([to_end, to_end], axis=1)
        both = mm3(split2(jnp.concatenate([qmix, kt], axis=0)), split2(wu))
        reads_ref[h, :, :DK] = (ecum * rq) * qf - both[:tok, :DK]
        reads_ref[h, :, DK:] = both[:tok, DK:]
        elast = jnp.exp(last)
        maps_ref[h, :, :DK] = jnp.where(row_t == col_t, elast, 0.0) - both[tok:, :DK]
        maps_ref[h, :, DK:] = both[tok:, DK:]


def final_kernel(heads, reads_ref, state_ref, gain_ref, w_ref, out_ref):
    parts = []
    for h in range(heads):
        att = reads_ref[h, :, DK:] + mm3(split2(reads_ref[h, :, :DK]), split2(state_ref[h]))
        inv = lax.rsqrt(jnp.mean(att * att, axis=-1, keepdims=True) + 1e-05)
        parts.append((att * inv * gain_ref[:, h * DV : (h + 1) * DV]).astype(BF16))
    out_ref[...] = dot1(jnp.concatenate(parts, axis=1), w_ref[...])


def batch_mm(left_mat, right_mat):
    return jnp.einsum("hij,hjk->hik", left_mat, right_mat, precision=lax.Precision.HIGHEST)


def compose_stack(earlier, later):
    later_trans = later[..., :DK]
    added = jnp.concatenate([jnp.zeros_like(later_trans), later[..., DK:]], axis=-1)
    return batch_mm(later_trans, earlier) + added


def paired_prefix(total_map, identity_map):
    seq_rank = lax.axis_index("seq")
    levels = lax.axis_size("seq").bit_length() - 1
    running = total_map
    before = identity_map
    for bit_pos in range(levels):
        partner = swapped(running, "seq", bit_pos)
        is_upper = seq_rank // 2**bit_pos % 2 == 1
        earlier_part = jnp.where(is_upper, partner, running)
        later_part = jnp.where(is_upper, running, partner)
        shifted = compose_stack(partner, before)
        before = jnp.where(is_upper, shifted, before)
        running = compose_stack(earlier_part, later_part)
    return before


def local_call(queries, keys2, vals2, small, heads):
    tok = queries.shape[0]
    vmem = pl.BlockSpec(memory_space=pltpu.VMEM)
    return pl.pallas_call(
        functools.partial(local_kernel, heads),
        out_shape=[jax.ShapeDtypeStruct((heads, DK, DK + DV), F32), jax.ShapeDtypeStruct((heads, tok, DK + DV), F32)],
        in_specs=[vmem] * 4,
        out_specs=[vmem] * 2,
        scratch_shapes=[
            pltpu.VMEM((heads, 2 * tok, 2 * tok), F32),
            pltpu.VMEM((heads, 2 * tok, 2 * tok), BF16),
            pltpu.VMEM((heads, 2 * tok, 2 * tok), BF16),
        ],
        compiler_params=pltpu.CompilerParams(vmem_limit_bytes=40 << 20),
        name="local_maps",
    )(queries, keys2, vals2, small)


def shards(queries, key_rows, value_rows, strengths, log_gate, keep_flag, norm_gain, out_weight):
    tok = queries.shape[0]
    heads = strengths.shape[0]
    live = keep_flag.astype(F32)[None, :]
    small = jnp.concatenate(
        [strengths[:, 0] * live, strengths[:, 1] * live, log_gate * live, jnp.zeros((heads, tok), F32)], axis=0
    )
    keys2 = key_rows.reshape(tok, -1)
    vals2 = value_rows.reshape(tok, -1)
    maps, reads = local_call(queries, keys2, vals2, small, heads)
    eye_heads = jnp.broadcast_to(jnp.eye(DK, dtype=F32), (heads, DK, DK))
    identity_map = jnp.concatenate([eye_heads, jnp.zeros((heads, DK, DV), F32)], axis=-1)
    state = paired_prefix(maps, identity_map)[..., DK:]
    vmem = pl.BlockSpec(memory_space=pltpu.VMEM)
    partial_out = pl.pallas_call(
        functools.partial(final_kernel, heads),
        out_shape=jax.ShapeDtypeStruct((tok, out_weight.shape[1]), F32),
        in_specs=[vmem] * 4,
        out_specs=vmem,
        compiler_params=pltpu.CompilerParams(vmem_limit_bytes=40 << 20),
        name="read_project",
    )(reads, state, norm_gain[None, :], out_weight)
    projected = lax.psum_scatter(partial_out, "head", scatter_dimension=0, tiled=True)
    return projected.astype(BF16)


def solution(mesh):
    in_specs = (
        P(("groups", "seq"), "head"),
        P(("groups", "seq"), None, "head"),
        P(("groups", "seq"), None, "head"),
        P("head", None, ("groups", "seq")),
        P("head", ("groups", "seq")),
        P(("groups", "seq")),
        P("head"),
        P("head", None),
    )
    out_specs = P(("groups", "seq", "head"), None)
    return jax.shard_map(shards, mesh=mesh, in_specs=in_specs, out_specs=out_specs, check_vma=False)
```

```python
import functools

import jax
import jax.numpy as jnp
from jax import lax
from jax.experimental import pallas as pl
from jax.experimental.pallas import tpu as pltpu
from jax.sharding import PartitionSpec as P

DK = 128
DV = 128
UNITS = 2
CHUNKS = 4
F32 = jnp.float32
BF16 = jnp.bfloat16


def split2(x):
    hi = x.astype(BF16)
    return hi, (x - hi.astype(F32)).astype(BF16)


def dot1(a, b):
    return jnp.dot(a, b, preferred_element_type=F32)


def mm3(a, b):
    return dot1(a[0], b[0]) + (dot1(a[0], b[1]) + dot1(a[1], b[0]))


def dot_nt(a, b):
    return lax.dot_general(a, b, (((1,), (1,)), ((), ())), preferred_element_type=F32)


def local_kernel(heads, q_ref, k_ref, v_ref, small_ref, maps_ref, reads_ref, a_sc, xh_sc, xl_sc):
    tok = q_ref.shape[0]
    size = 2 * tok
    width = heads * DK
    row_t = lax.broadcasted_iota(jnp.int32, (tok, tok), 0)
    col_t = lax.broadcasted_iota(jnp.int32, (tok, tok), 1)
    incl = row_t >= col_t
    strict = row_t > col_t
    small = small_ref[...]
    s1 = small.astype(BF16)
    rest = small - s1.astype(F32)
    s2 = rest.astype(BF16)
    s3 = (rest - s2.astype(F32)).astype(BF16)
    upper = jnp.where(row_t <= col_t, 1.0, 0.0).astype(BF16)
    cum = dot1(s1, upper) + (dot1(s2, upper) + dot1(s3, upper))
    srows = small.shape[0]
    cols = jnp.concatenate([small, cum, jnp.zeros((tok - 2 * srows, tok), F32)], axis=0).T

    row_i = lax.broadcasted_iota(jnp.int32, (size, size), 0)
    col_i = lax.broadcasted_iota(jnp.int32, (size, size), 1)
    time_r = jnp.where(row_i < tok, 2 * row_i, 2 * row_i - 2 * tok + 1)
    time_c = jnp.where(col_i < tok, 2 * col_i, 2 * col_i - 2 * tok + 1)

    for h in range(heads):
        kk = [k_ref[:, j * width + h * DK : j * width + (h + 1) * DK] for j in range(2)]
        keys = jnp.concatenate(kk, axis=0)
        gram = dot_nt(keys, keys)
        cum_col = cols[:, srows + 2 * heads + h : srows + 2 * heads + h + 1]
        cum_row = cum[2 * heads + h : 2 * heads + h + 1, :]
        decay = jnp.where(incl, jnp.exp(jnp.where(incl, cum_col - cum_row, 0.0)), 0.0)
        decay_s = jnp.where(strict, decay, 0.0)
        kf = keys.astype(F32)
        r2 = 1.0 / (jnp.sum(kf * kf, axis=-1, keepdims=True) + 1e-06)
        beta = jnp.concatenate([cols[:, h : h + 1], cols[:, heads + h : heads + h + 1]], axis=0)
        factor = jnp.concatenate(
            [jnp.concatenate([decay_s, decay_s], axis=1), jnp.concatenate([decay, decay_s], axis=1)], axis=0
        )
        a_full = (beta * r2) * factor * gram
        a_sc[h] = a_full
        first = jnp.where((time_r ^ time_c) == 1, a_full, 0.0)
        x0 = jnp.where(time_r == time_c, 1.0, 0.0) - first
        xh_sc[h], xl_sc[h] = split2(x0)

    bit = 1
    while 2 << bit <= size:
        low = time_c >> bit
        picked = ((time_r >> bit) == (low | 1)) & ((low & 1) == 0)
        for h in range(heads):
            b = split2(jnp.where(picked, a_sc[h], 0.0))
            x = (xh_sc[h], xl_sc[h])
            y = split2(mm3(b, x))
            d = split2(mm3(x, y))
            xh_sc[h] = x[0] - d[0]
            xl_sc[h] = x[1] - d[1]
        bit += 1

    for h in range(heads):
        kk = [k_ref[:, j * width + h * DK : j * width + (h + 1) * DK] for j in range(2)]
        vv = [v_ref[:, j * width + h * DV : j * width + (h + 1) * DV] for j in range(2)]
        keys = jnp.concatenate(kk, axis=0)
        vals = jnp.concatenate(vv, axis=0).astype(F32)
        kf = keys.astype(F32)
        ss = jnp.sum(kf * kf, axis=-1, keepdims=True) + 1e-06
        beta = jnp.concatenate([cols[:, h : h + 1], cols[:, heads + h : heads + h + 1]], axis=0)
        cum_col = cols[:, srows + 2 * heads + h : srows + 2 * heads + h + 1]
        cum_row = cum[2 * heads + h : 2 * heads + h + 1, :]
        ecum = jnp.exp(cum_col)
        ecum2 = jnp.concatenate([ecum, ecum], axis=0)
        rhs = jnp.concatenate([(beta * ecum2 / ss) * kf, (beta * lax.rsqrt(ss)) * vals], axis=1)
        wu = mm3((xh_sc[h], xl_sc[h]), split2(rhs))
        q = q_ref[:, h * DK : (h + 1) * DK]
        qf = q.astype(F32)
        rq = lax.rsqrt(jnp.sum(qf * qf, axis=-1, keepdims=True) + 1e-06)
        decay = jnp.where(incl, jnp.exp(jnp.where(incl, cum_col - cum_row, 0.0)), 0.0)
        qmix = jnp.concatenate([decay, decay], axis=1) * (rq * dot_nt(q, keys))
        last = cum_row[:, tok - 1 : tok]
        to_end = jnp.exp(last - cum_row)
        kt = kf.T * jnp.concatenate([to_end, to_end], axis=1)
        both = mm3(split2(jnp.concatenate([qmix, kt], axis=0)), split2(wu))
        reads_ref[h, :, :DK] = (ecum * rq) * qf - both[:tok, :DK]
        reads_ref[h, :, DK:] = both[:tok, DK:]
        elast = jnp.exp(last)
        maps_ref[h, :, :DK] = jnp.where(row_t == col_t, elast, 0.0) - both[tok:, :DK].T
        maps_ref[h, :, DK:] = both[tok:, DK:].T


def chain_kernel(
    heads, maps_ref, reads_ref, gain_ref, w_ref, out_ref,
    sin, sout, th_sc, tl_sc, nrm, part, other, send_sem, recv_sem, xsend, xrecv,
):
    n = lax.axis_size("seq")
    me = lax.axis_index("seq")
    core = lax.axis_index("head")
    sibling = 1 - core
    right = lax.rem(me + 1, n)
    barrier = pltpu.get_barrier_semaphore()

    def signal(where):
        pl.semaphore_signal(barrier, inc=1, device_id=where, device_id_type=pl.DeviceIdType.MESH)

    signal({"head": sibling})

    @pl.when(me < n - 1)
    def _():
        signal({"seq": right})

    @pl.when(me > 0)
    def _():
        signal({"seq": lax.rem(me + n - 1, n)})

    for h in range(heads):
        th_sc[h], tl_sc[h] = split2(maps_ref[h, :, :DK])
    inner = (me > 0) & (me < n - 1)

    @pl.when(inner)
    def _():
        pl.semaphore_wait(barrier, 3)

    @pl.when(jnp.logical_not(inner))
    def _():
        pl.semaphore_wait(barrier, 2)

    rows = DV // UNITS

    def hop(h, u):
        span = pl.ds(u * rows, rows)
        return pltpu.make_async_remote_copy(
            src_ref=sout.at[h, span],
            dst_ref=sin.at[h, span],
            send_sem=send_sem.at[h * UNITS + u],
            recv_sem=recv_sem.at[h * UNITS + u],
            device_id={"seq": right},
            device_id_type=pl.DeviceIdType.MESH,
        )

    for h in range(heads):
        for u in range(UNITS):
            lo, hi = u * rows, (u + 1) * rows

            @pl.when(me == 0)
            def _():
                sin[h, lo:hi] = jnp.zeros((rows, DK), F32)
                sout[h, lo:hi] = maps_ref[h, lo:hi, DK:]

            @pl.when(me > 0)
            def _():
                hop(h, u).wait_recv()
                moved = mm3(split2(sin[h, lo:hi]), (th_sc[h], tl_sc[h]))
                sout[h, lo:hi] = moved + maps_ref[h, lo:hi, DK:]

            @pl.when(me < n - 1)
            def _():
                hop(h, u).start()

    for h in range(heads):
        state = split2(sin[h])
        reach = split2(reads_ref[h, :, :DK])
        seen = dot_nt(reach[0], state[0]) + (dot_nt(reach[0], state[1]) + dot_nt(reach[1], state[0]))
        att = reads_ref[h, :, DK:] + seen
        inv = lax.rsqrt(jnp.mean(att * att, axis=-1, keepdims=True) + 1e-05)
        nrm[:, h * DV : (h + 1) * DV] = (att * inv * gain_ref[:, h * DV : (h + 1) * DV]).astype(BF16)

    half = nrm.shape[0] // 2
    wide = part.shape[-1]
    chunks = part.shape[0]

    def cross(c):
        return pltpu.make_async_remote_copy(
            src_ref=part.at[c],
            dst_ref=other.at[c],
            send_sem=xsend.at[c],
            recv_sem=xrecv.at[c],
            device_id={"head": sibling},
            device_id_type=pl.DeviceIdType.MESH,
        )

    theirs = nrm[pl.ds(pl.multiple_of(sibling * half, half), half), :]
    for c in range(chunks):
        part[c] = dot1(theirs, w_ref[:, c * wide : (c + 1) * wide])
        cross(c).start()
    mine = nrm[pl.ds(pl.multiple_of(core * half, half), half), :]
    for c in range(chunks):
        own = dot1(mine, w_ref[:, c * wide : (c + 1) * wide])
        cross(c).wait_recv()
        out_ref[:, c * wide : (c + 1) * wide] = (own + other[c]).astype(BF16)
    for c in range(chunks):
        cross(c).wait_send()

    @pl.when(me < n - 1)
    def _():
        for h in range(heads):
            for u in range(UNITS):
                hop(h, u).wait_send()


def local_call(queries, keys2, vals2, small, heads):
    tok = queries.shape[0]
    vmem = pl.BlockSpec(memory_space=pltpu.VMEM)
    return pl.pallas_call(
        functools.partial(local_kernel, heads),
        out_shape=[jax.ShapeDtypeStruct((heads, DK, DK + DV), F32), jax.ShapeDtypeStruct((heads, tok, DK + DV), F32)],
        in_specs=[vmem] * 4,
        out_specs=[vmem] * 2,
        scratch_shapes=[
            pltpu.VMEM((heads, 2 * tok, 2 * tok), F32),
            pltpu.VMEM((heads, 2 * tok, 2 * tok), BF16),
            pltpu.VMEM((heads, 2 * tok, 2 * tok), BF16),
        ],
        compiler_params=pltpu.CompilerParams(vmem_limit_bytes=40 << 20),
        name="local_maps",
    )(queries, keys2, vals2, small)


def shards(queries, key_rows, value_rows, strengths, log_gate, keep_flag, norm_gain, out_weight):
    tok = queries.shape[0]
    heads = strengths.shape[0]
    live = keep_flag.astype(F32)[None, :]
    small = jnp.concatenate(
        [strengths[:, 0] * live, strengths[:, 1] * live, log_gate * live, jnp.zeros((heads, tok), F32)], axis=0
    )
    keys2 = key_rows.reshape(tok, -1)
    vals2 = value_rows.reshape(tok, -1)
    maps, reads = local_call(queries, keys2, vals2, small, heads)
    vmem = pl.BlockSpec(memory_space=pltpu.VMEM)
    wide = out_weight.shape[1]
    return pl.pallas_call(
        functools.partial(chain_kernel, heads),
        out_shape=jax.ShapeDtypeStruct((tok // 2, wide), BF16),
        in_specs=[vmem] * 4,
        out_specs=vmem,
        scratch_shapes=[
            pltpu.VMEM((heads, DV, DK), F32),
            pltpu.VMEM((heads, DV, DK), F32),
            pltpu.VMEM((heads, DK, DK), BF16),
            pltpu.VMEM((heads, DK, DK), BF16),
            pltpu.VMEM((tok, heads * DV), BF16),
            pltpu.VMEM((CHUNKS, tok // 2, wide // CHUNKS), F32),
            pltpu.VMEM((CHUNKS, tok // 2, wide // CHUNKS), F32),
            pltpu.SemaphoreType.DMA((heads * UNITS,)),
            pltpu.SemaphoreType.DMA((heads * UNITS,)),
            pltpu.SemaphoreType.DMA((CHUNKS,)),
            pltpu.SemaphoreType.DMA((CHUNKS,)),
        ],
        compiler_params=pltpu.CompilerParams(vmem_limit_bytes=40 << 20, collective_id=0, has_side_effects=True),
        name="chain_project",
    )(maps, reads, norm_gain[None, :], out_weight)


def solution(mesh):
    in_specs = (
        P(("groups", "seq"), "head"),
        P(("groups", "seq"), None, "head"),
        P(("groups", "seq"), None, "head"),
        P("head", None, ("groups", "seq")),
        P("head", ("groups", "seq")),
        P(("groups", "seq")),
        P("head"),
        P("head", None),
    )
    out_specs = P(("groups", "seq", "head"), None)
    return jax.shard_map(shards, mesh=mesh, in_specs=in_specs, out_specs=out_specs, check_vma=False)
```

```python
import functools

import jax
import jax.numpy as jnp
from jax import lax
from jax.experimental import pallas as pl
from jax.experimental.pallas import tpu as pltpu
from jax.sharding import PartitionSpec as P

DK = 128
DV = 128
UNITS = 4
CHUNKS = 4
F32 = jnp.float32
BF16 = jnp.bfloat16


def split2(x):
    hi = x.astype(BF16)
    return hi, (x - hi.astype(F32)).astype(BF16)


def dot1(a, b):
    return jnp.dot(a, b, preferred_element_type=F32)


def mm3(a, b):
    return dot1(a[0], b[0]) + (dot1(a[0], b[1]) + dot1(a[1], b[0]))


def dot_nt(a, b):
    return lax.dot_general(a, b, (((1,), (1,)), ((), ())), preferred_element_type=F32)


def local_maps(
    heads, loads, k_ref, v_ref, bias_ref, th_sc, tl_sc, reads_ref,
    a_sc, xh_sc, xl_sc, small_ref, q_ref, str_ref, log_ref, keep_ref,
):
    tok = q_ref.shape[0]
    for load in loads[:3]:
        load.wait()
    live = keep_ref[...].astype(F32)
    small_ref[...] = jnp.zeros_like(small_ref)
    small_ref[:heads] = str_ref[:, 0, :] * live
    small_ref[heads : 2 * heads] = str_ref[:, 1, :] * live
    small_ref[2 * heads : 3 * heads] = log_ref[...] * live
    size = 2 * tok
    width = heads * DK
    row_t = lax.broadcasted_iota(jnp.int32, (tok, tok), 0)
    col_t = lax.broadcasted_iota(jnp.int32, (tok, tok), 1)
    incl = row_t >= col_t
    strict = row_t > col_t
    small = small_ref[...]
    s1 = small.astype(BF16)
    rest = small - s1.astype(F32)
    s2 = rest.astype(BF16)
    s3 = (rest - s2.astype(F32)).astype(BF16)
    upper = jnp.where(row_t <= col_t, 1.0, 0.0).astype(BF16)
    cum = dot1(s1, upper) + (dot1(s2, upper) + dot1(s3, upper))
    srows = small.shape[0]
    cols = jnp.concatenate([small, cum, jnp.zeros((tok - 2 * srows, tok), F32)], axis=0).T

    row_i = lax.broadcasted_iota(jnp.int32, (size, size), 0)
    col_i = lax.broadcasted_iota(jnp.int32, (size, size), 1)
    time_r = jnp.where(row_i < tok, 2 * row_i, 2 * row_i - 2 * tok + 1)
    time_c = jnp.where(col_i < tok, 2 * col_i, 2 * col_i - 2 * tok + 1)

    for h in range(heads):
        kk = [k_ref[:, j * width + h * DK : j * width + (h + 1) * DK] for j in range(2)]
        keys = jnp.concatenate(kk, axis=0)
        gram = dot_nt(keys, keys)
        cum_col = cols[:, srows + 2 * heads + h : srows + 2 * heads + h + 1]
        cum_row = cum[2 * heads + h : 2 * heads + h + 1, :]
        decay = jnp.where(incl, jnp.exp(jnp.where(incl, cum_col - cum_row, 0.0)), 0.0)
        decay_s = jnp.where(strict, decay, 0.0)
        kf = keys.astype(F32)
        r2 = 1.0 / (jnp.sum(kf * kf, axis=-1, keepdims=True) + 1e-06)
        beta = jnp.concatenate([cols[:, h : h + 1], cols[:, heads + h : heads + h + 1]], axis=0)
        factor = jnp.concatenate(
            [jnp.concatenate([decay_s, decay_s], axis=1), jnp.concatenate([decay, decay_s], axis=1)], axis=0
        )
        a_full = (beta * r2) * factor * gram
        a_sc[h] = a_full
        first = jnp.where((time_r ^ time_c) == 1, a_full, 0.0)
        x0 = jnp.where(time_r == time_c, 1.0, 0.0) - first
        xh_sc[h], xl_sc[h] = split2(x0)

    bit = 1
    while 2 << bit <= size:
        low = time_c >> bit
        picked = ((time_r >> bit) == (low | 1)) & ((low & 1) == 0)
        for h in range(heads):
            b = split2(jnp.where(picked, a_sc[h], 0.0))
            x = (xh_sc[h], xl_sc[h])
            y = split2(mm3(b, x))
            d = split2(mm3(x, y))
            xh_sc[h] = x[0] - d[0]
            xl_sc[h] = x[1] - d[1]
        bit += 1

    loads[3].wait()
    for h in range(heads):
        kk = [k_ref[:, j * width + h * DK : j * width + (h + 1) * DK] for j in range(2)]
        vv = [v_ref[:, j * width + h * DV : j * width + (h + 1) * DV] for j in range(2)]
        keys = jnp.concatenate(kk, axis=0)
        vals = jnp.concatenate(vv, axis=0).astype(F32)
        kf = keys.astype(F32)
        ss = jnp.sum(kf * kf, axis=-1, keepdims=True) + 1e-06
        beta = jnp.concatenate([cols[:, h : h + 1], cols[:, heads + h : heads + h + 1]], axis=0)
        cum_col = cols[:, srows + 2 * heads + h : srows + 2 * heads + h + 1]
        cum_row = cum[2 * heads + h : 2 * heads + h + 1, :]
        ecum = jnp.exp(cum_col)
        ecum2 = jnp.concatenate([ecum, ecum], axis=0)
        rhs = jnp.concatenate([(beta * ecum2 / ss) * kf, (beta * lax.rsqrt(ss)) * vals], axis=1)
        wu = mm3((xh_sc[h], xl_sc[h]), split2(rhs))
        q = q_ref[:, h * DK : (h + 1) * DK]
        qf = q.astype(F32)
        rq = lax.rsqrt(jnp.sum(qf * qf, axis=-1, keepdims=True) + 1e-06)
        decay = jnp.where(incl, jnp.exp(jnp.where(incl, cum_col - cum_row, 0.0)), 0.0)
        qmix = jnp.concatenate([decay, decay], axis=1) * (rq * dot_nt(q, keys))
        last = cum_row[:, tok - 1 : tok]
        to_end = jnp.exp(last - cum_row)
        kt = kf.T * jnp.concatenate([to_end, to_end], axis=1)
        both = mm3(split2(jnp.concatenate([qmix, kt], axis=0)), split2(wu))
        reads_ref[h, :, :DK] = (ecum * rq) * qf - both[:tok, :DK]
        reads_ref[h, :, DK:] = both[:tok, DK:]
        elast = jnp.exp(last)
        th_sc[h], tl_sc[h] = split2(jnp.where(row_t == col_t, elast, 0.0) - both[tok:, :DK].T)
        bias_ref[h] = both[tok:, DK:].T


def chain_kernel(
    heads, q_hbm, k_ref, v_ref, str_hbm, log_hbm, keep_hbm, gain_hbm, w_hbm, out_ref,
    a_sc, xh_sc, xl_sc, small_ref, q_ref, str_ref, log_ref, keep_ref,
    gain_ref, w_ref, load_sem, bias_ref, reads_ref, sin, sout, th_sc, tl_sc, nrm, part, other, send_sem, recv_sem, xsend, xrecv,
):
    pairs = (
        (str_hbm, str_ref),
        (log_hbm, log_ref),
        (keep_hbm, keep_ref),
        (q_hbm, q_ref),
        (gain_hbm, gain_ref),
        (w_hbm, w_ref),
    )
    loads = [pltpu.make_async_copy(a, b, load_sem.at[i]) for i, (a, b) in enumerate(pairs)]
    for load in loads:
        load.start()
    n = lax.axis_size("seq")
    me = lax.axis_index("seq")
    core = lax.axis_index("head")
    sibling = 1 - core
    right = lax.rem(me + 1, n)
    barrier = pltpu.get_barrier_semaphore()

    def signal(where):
        pl.semaphore_signal(barrier, inc=1, device_id=where, device_id_type=pl.DeviceIdType.MESH)

    signal({"head": sibling})

    @pl.when(me < n - 1)
    def _():
        signal({"seq": right})

    @pl.when(me > 0)
    def _():
        signal({"seq": lax.rem(me + n - 1, n)})

    local_maps(
        heads, loads, k_ref, v_ref, bias_ref, th_sc, tl_sc, reads_ref,
        a_sc, xh_sc, xl_sc, small_ref, q_ref, str_ref, log_ref, keep_ref,
    )
    inner = (me > 0) & (me < n - 1)

    @pl.when(inner)
    def _():
        pl.semaphore_wait(barrier, 3)

    @pl.when(jnp.logical_not(inner))
    def _():
        pl.semaphore_wait(barrier, 2)

    rows = DV // UNITS

    def hop(h, u):
        span = pl.ds(u * rows, rows)
        return pltpu.make_async_remote_copy(
            src_ref=sout.at[h, span],
            dst_ref=sin.at[h, span],
            send_sem=send_sem.at[h * UNITS + u],
            recv_sem=recv_sem.at[h * UNITS + u],
            device_id={"seq": right},
            device_id_type=pl.DeviceIdType.MESH,
        )

    def read(h):
        state = split2(sin[h])
        reach = split2(reads_ref[h, :, :DK])
        seen = dot_nt(reach[0], state[0]) + (dot_nt(reach[0], state[1]) + dot_nt(reach[1], state[0]))
        att = reads_ref[h, :, DK:] + seen
        inv = lax.rsqrt(jnp.mean(att * att, axis=-1, keepdims=True) + 1e-05)
        nrm[:, h * DV : (h + 1) * DV] = (att * inv * gain_ref[:, h * DV : (h + 1) * DV]).astype(BF16)

    loads[4].wait()
    for h in range(heads):
        for u in range(UNITS):
            lo, hi = u * rows, (u + 1) * rows

            @pl.when(me == 0)
            def _():
                sin[h, lo:hi] = jnp.zeros((rows, DK), F32)
                sout[h, lo:hi] = bias_ref[h, lo:hi]

            @pl.when(me > 0)
            def _():
                hop(h, u).wait_recv()

            @pl.when(inner)
            def _():
                moved = mm3(split2(sin[h, lo:hi]), (th_sc[h], tl_sc[h]))
                sout[h, lo:hi] = moved + bias_ref[h, lo:hi]

            @pl.when(me < n - 1)
            def _():
                hop(h, u).start()

        @pl.when(me == n - 1)
        def _():
            read(h)

    @pl.when(me < n - 1)
    def _():
        for h in range(heads):
            read(h)

    loads[5].wait()
    half = nrm.shape[0] // 2
    wide = part.shape[-1]
    chunks = part.shape[0]

    def cross(c):
        return pltpu.make_async_remote_copy(
            src_ref=part.at[c],
            dst_ref=other.at[c],
            send_sem=xsend.at[c],
            recv_sem=xrecv.at[c],
            device_id={"head": sibling},
            device_id_type=pl.DeviceIdType.MESH,
        )

    theirs = nrm[pl.ds(pl.multiple_of(sibling * half, half), half), :]
    for c in range(chunks):
        part[c] = dot1(theirs, w_ref[:, c * wide : (c + 1) * wide])
        cross(c).start()
    mine = nrm[pl.ds(pl.multiple_of(core * half, half), half), :]
    for c in range(chunks):
        own = dot1(mine, w_ref[:, c * wide : (c + 1) * wide])
        cross(c).wait_recv()
        out_ref[:, c * wide : (c + 1) * wide] = (own + other[c]).astype(BF16)
    for c in range(chunks):
        cross(c).wait_send()

    @pl.when(me < n - 1)
    def _():
        for h in range(heads):
            for u in range(UNITS):
                hop(h, u).wait_send()


def shards(queries, key_rows, value_rows, strengths, log_gate, keep_flag, norm_gain, out_weight):
    tok = queries.shape[0]
    heads = strengths.shape[0]
    keys2 = key_rows.reshape(tok, -1)
    vals2 = value_rows.reshape(tok, -1)
    vmem = pl.BlockSpec(memory_space=pltpu.VMEM)
    hbm = pl.BlockSpec(memory_space=pltpu.HBM)
    wide = out_weight.shape[1]
    return pl.pallas_call(
        functools.partial(chain_kernel, heads),
        out_shape=jax.ShapeDtypeStruct((tok // 2, wide), BF16),
        in_specs=[hbm, vmem, vmem, hbm, hbm, hbm, hbm, hbm],
        out_specs=vmem,
        scratch_shapes=[
            pltpu.VMEM((heads, 2 * tok, 2 * tok), F32),
            pltpu.VMEM((heads, 2 * tok, 2 * tok), BF16),
            pltpu.VMEM((heads, 2 * tok, 2 * tok), BF16),
            pltpu.VMEM((4 * heads, tok), F32),
            pltpu.VMEM(queries.shape, BF16),
            pltpu.VMEM(strengths.shape, F32),
            pltpu.VMEM(log_gate.shape, F32),
            pltpu.VMEM((1, tok), jnp.int32),
            pltpu.VMEM((1, heads * DV), F32),
            pltpu.VMEM(out_weight.shape, BF16),
            pltpu.SemaphoreType.DMA((6,)),
            pltpu.VMEM((heads, DV, DK), F32),
            pltpu.VMEM((heads, tok, DK + DV), F32),
            pltpu.VMEM((heads, DV, DK), F32),
            pltpu.VMEM((heads, DV, DK), F32),
            pltpu.VMEM((heads, DK, DK), BF16),
            pltpu.VMEM((heads, DK, DK), BF16),
            pltpu.VMEM((tok, heads * DV), BF16),
            pltpu.VMEM((CHUNKS, tok // 2, wide // CHUNKS), F32),
            pltpu.VMEM((CHUNKS, tok // 2, wide // CHUNKS), F32),
            pltpu.SemaphoreType.DMA((heads * UNITS,)),
            pltpu.SemaphoreType.DMA((heads * UNITS,)),
            pltpu.SemaphoreType.DMA((CHUNKS,)),
            pltpu.SemaphoreType.DMA((CHUNKS,)),
        ],
        compiler_params=pltpu.CompilerParams(vmem_limit_bytes=62 << 20, collective_id=0, has_side_effects=True),
        name="chain_project",
    )(queries, keys2, vals2, strengths, log_gate, keep_flag[None, :], norm_gain[None, :], out_weight)


def solution(mesh):
    in_specs = (
        P(("groups", "seq"), "head"),
        P(("groups", "seq"), None, "head"),
        P(("groups", "seq"), None, "head"),
        P("head", None, ("groups", "seq")),
        P("head", ("groups", "seq")),
        P(("groups", "seq")),
        P("head"),
        P("head", None),
    )
    out_specs = P(("groups", "seq", "head"), None)
    return jax.shard_map(shards, mesh=mesh, in_specs=in_specs, out_specs=out_specs, check_vma=False)
```

```python
import functools

import jax
import jax.numpy as jnp
from jax import lax
from jax.experimental import pallas as pl
from jax.experimental.pallas import tpu as pltpu
from jax.sharding import PartitionSpec as P

DK = 128
DV = 128
UNITS = 4
GROUP = 2
CHUNKS = 4
F32 = jnp.float32
BF16 = jnp.bfloat16


def split2(x):
    hi = x.astype(BF16)
    return hi, (x - hi.astype(F32)).astype(BF16)


def dot1(a, b):
    return jnp.dot(a, b, preferred_element_type=F32)


def mm3(a, b):
    return dot1(a[0], b[0]) + (dot1(a[0], b[1]) + dot1(a[1], b[0]))


def dot_nt(a, b):
    return lax.dot_general(a, b, (((1,), (1,)), ((), ())), preferred_element_type=F32)


def local_maps(
    heads, loads, k_ref, v_ref, bias_ref, th_sc, tl_sc, reads_ref,
    a_sc, xh_sc, xl_sc, small_ref, q_ref, str_ref, log_ref, keep_ref,
):
    tok = q_ref.shape[0]
    for load in loads[:4]:
        load.wait()
    live = keep_ref[...].astype(F32)
    small_ref[...] = jnp.zeros_like(small_ref)
    small_ref[:heads] = str_ref[:, 0, :] * live
    small_ref[heads : 2 * heads] = str_ref[:, 1, :] * live
    small_ref[2 * heads : 3 * heads] = log_ref[...] * live
    size = 2 * tok
    width = heads * DK
    row_t = lax.broadcasted_iota(jnp.int32, (tok, tok), 0)
    col_t = lax.broadcasted_iota(jnp.int32, (tok, tok), 1)
    incl = row_t >= col_t
    strict = row_t > col_t
    small = small_ref[...]
    s1 = small.astype(BF16)
    rest = small - s1.astype(F32)
    s2 = rest.astype(BF16)
    s3 = (rest - s2.astype(F32)).astype(BF16)
    upper = jnp.where(row_t <= col_t, 1.0, 0.0).astype(BF16)
    cum = dot1(s1, upper) + (dot1(s2, upper) + dot1(s3, upper))
    srows = small.shape[0]
    cols = jnp.concatenate([small, cum, jnp.zeros((tok - 2 * srows, tok), F32)], axis=0).T

    row_i = lax.broadcasted_iota(jnp.int32, (size, size), 0)
    col_i = lax.broadcasted_iota(jnp.int32, (size, size), 1)
    time_r = jnp.where(row_i < tok, 2 * row_i, 2 * row_i - 2 * tok + 1)
    time_c = jnp.where(col_i < tok, 2 * col_i, 2 * col_i - 2 * tok + 1)

    def run(group):
        for h in group:
            kk = [k_ref[:, j * width + h * DK : j * width + (h + 1) * DK] for j in range(2)]
            keys = jnp.concatenate(kk, axis=0)
            gram = dot_nt(keys, keys)
            cum_col = cols[:, srows + 2 * heads + h : srows + 2 * heads + h + 1]
            cum_row = cum[2 * heads + h : 2 * heads + h + 1, :]
            decay = jnp.where(incl, jnp.exp(jnp.where(incl, cum_col - cum_row, 0.0)), 0.0)
            decay_s = jnp.where(strict, decay, 0.0)
            kf = keys.astype(F32)
            r2 = 1.0 / (jnp.sum(kf * kf, axis=-1, keepdims=True) + 1e-06)
            beta = jnp.concatenate([cols[:, h : h + 1], cols[:, heads + h : heads + h + 1]], axis=0)
            factor = jnp.concatenate(
                [jnp.concatenate([decay_s, decay_s], axis=1), jnp.concatenate([decay, decay_s], axis=1)], axis=0
            )
            a_full = (beta * r2) * factor * gram
            a_sc[h] = a_full
            first = jnp.where((time_r ^ time_c) == 1, a_full, 0.0)
            x0 = jnp.where(time_r == time_c, 1.0, 0.0) - first
            xh_sc[h], xl_sc[h] = split2(x0)

        bit = 1
        while 2 << bit <= size:
            low = time_c >> bit
            picked = ((time_r >> bit) == (low | 1)) & ((low & 1) == 0)
            for h in group:
                b = split2(jnp.where(picked, a_sc[h], 0.0))
                x = (xh_sc[h], xl_sc[h])
                y = split2(mm3(b, x))
                d = split2(mm3(x, y))
                xh_sc[h] = x[0] - d[0]
                xl_sc[h] = x[1] - d[1]
            bit += 1

        for h in group:
            kk = [k_ref[:, j * width + h * DK : j * width + (h + 1) * DK] for j in range(2)]
            vv = [v_ref[:, j * width + h * DV : j * width + (h + 1) * DV] for j in range(2)]
            keys = jnp.concatenate(kk, axis=0)
            vals = jnp.concatenate(vv, axis=0).astype(F32)
            kf = keys.astype(F32)
            ss = jnp.sum(kf * kf, axis=-1, keepdims=True) + 1e-06
            beta = jnp.concatenate([cols[:, h : h + 1], cols[:, heads + h : heads + h + 1]], axis=0)
            cum_col = cols[:, srows + 2 * heads + h : srows + 2 * heads + h + 1]
            cum_row = cum[2 * heads + h : 2 * heads + h + 1, :]
            ecum = jnp.exp(cum_col)
            ecum2 = jnp.concatenate([ecum, ecum], axis=0)
            rhs = jnp.concatenate([(beta * ecum2 / ss) * kf, (beta * lax.rsqrt(ss)) * vals], axis=1)
            wu = mm3((xh_sc[h], xl_sc[h]), split2(rhs))
            q = q_ref[:, h * DK : (h + 1) * DK]
            qf = q.astype(F32)
            rq = lax.rsqrt(jnp.sum(qf * qf, axis=-1, keepdims=True) + 1e-06)
            decay = jnp.where(incl, jnp.exp(jnp.where(incl, cum_col - cum_row, 0.0)), 0.0)
            qmix = jnp.concatenate([decay, decay], axis=1) * (rq * dot_nt(q, keys))
            last = cum_row[:, tok - 1 : tok]
            to_end = jnp.exp(last - cum_row)
            kt = kf.T * jnp.concatenate([to_end, to_end], axis=1)
            both = mm3(split2(jnp.concatenate([qmix, kt], axis=0)), split2(wu))
            reads_ref[h, :, :DK] = (ecum * rq) * qf - both[:tok, :DK]
            reads_ref[h, :, DK:] = both[:tok, DK:]
            elast = jnp.exp(last)
            th_sc[h], tl_sc[h] = split2(jnp.where(row_t == col_t, elast, 0.0) - both[tok:, :DK].T)
            bias_ref[h] = both[tok:, DK:].T

    return run


def chain_kernel(
    heads, q_hbm, k_ref, v_ref, str_hbm, log_hbm, keep_hbm, gain_hbm, w_hbm, out_ref,
    a_sc, xh_sc, xl_sc, small_ref, q_ref, str_ref, log_ref, keep_ref,
    gain_ref, w_ref, load_sem, bias_ref, reads_ref, sin, sout, th_sc, tl_sc, nrm, part, other, send_sem, recv_sem, xsend, xrecv,
):
    pairs = (
        (str_hbm, str_ref),
        (log_hbm, log_ref),
        (keep_hbm, keep_ref),
        (q_hbm, q_ref),
        (gain_hbm, gain_ref),
        (w_hbm, w_ref),
    )
    loads = [pltpu.make_async_copy(a, b, load_sem.at[i]) for i, (a, b) in enumerate(pairs)]
    for load in loads:
        load.start()
    n = lax.axis_size("seq")
    me = lax.axis_index("seq")
    core = lax.axis_index("head")
    sibling = 1 - core
    right = lax.rem(me + 1, n)
    barrier = pltpu.get_barrier_semaphore()

    def signal(where):
        pl.semaphore_signal(barrier, inc=1, device_id=where, device_id_type=pl.DeviceIdType.MESH)

    signal({"head": sibling})

    @pl.when(me < n - 1)
    def _():
        signal({"seq": right})

    @pl.when(me > 0)
    def _():
        signal({"seq": lax.rem(me + n - 1, n)})

    run = local_maps(
        heads, loads, k_ref, v_ref, bias_ref, th_sc, tl_sc, reads_ref,
        a_sc, xh_sc, xl_sc, small_ref, q_ref, str_ref, log_ref, keep_ref,
    )

    rows = DV // UNITS

    def hop(h, u, src=None):
        span = pl.ds(u * rows, rows)
        return pltpu.make_async_remote_copy(
            src_ref=(sout if src is None else src).at[h, span],
            dst_ref=sin.at[h, span],
            send_sem=send_sem.at[h * UNITS + u],
            recv_sem=recv_sem.at[h * UNITS + u],
            device_id={"seq": right},
            device_id_type=pl.DeviceIdType.MESH,
        )

    inner = (me > 0) & (me < n - 1)
    for g in range(0, heads, GROUP):
        group = range(g, min(g + GROUP, heads))
        run(group)
        if g == 0:

            @pl.when(inner)
            def _():
                pl.semaphore_wait(barrier, 3)

            @pl.when(jnp.logical_not(inner))
            def _():
                pl.semaphore_wait(barrier, 2)

        @pl.when(me == 0)
        def _():
            for h in group:
                for u in range(UNITS):
                    hop(h, u, bias_ref).start()
                sin[h] = jnp.zeros((DV, DK), F32)

    def read(h):
        state = split2(sin[h])
        reach = split2(reads_ref[h, :, :DK])
        seen = dot_nt(reach[0], state[0]) + (dot_nt(reach[0], state[1]) + dot_nt(reach[1], state[0]))
        att = reads_ref[h, :, DK:] + seen
        inv = lax.rsqrt(jnp.mean(att * att, axis=-1, keepdims=True) + 1e-05)
        nrm[:, h * DV : (h + 1) * DV] = (att * inv * gain_ref[:, h * DV : (h + 1) * DV]).astype(BF16)

    loads[4].wait()
    for h in range(heads):
        for u in range(UNITS):
            lo, hi = u * rows, (u + 1) * rows

            @pl.when(me > 0)
            def _():
                hop(h, u).wait_recv()

            @pl.when(inner)
            def _():
                moved = mm3(split2(sin[h, lo:hi]), (th_sc[h], tl_sc[h]))
                sout[h, lo:hi] = moved + bias_ref[h, lo:hi]

            @pl.when(inner)
            def _():
                hop(h, u).start()

        @pl.when(me == n - 1)
        def _():
            read(h)

    @pl.when(me < n - 1)
    def _():
        for h in range(heads):
            read(h)

    loads[5].wait()
    half = nrm.shape[0] // 2
    wide = part.shape[-1]
    chunks = part.shape[0]

    def cross(c):
        return pltpu.make_async_remote_copy(
            src_ref=part.at[c],
            dst_ref=other.at[c],
            send_sem=xsend.at[c],
            recv_sem=xrecv.at[c],
            device_id={"head": sibling},
            device_id_type=pl.DeviceIdType.MESH,
        )

    theirs = nrm[pl.ds(pl.multiple_of(sibling * half, half), half), :]
    for c in range(chunks):
        part[c] = dot1(theirs, w_ref[:, c * wide : (c + 1) * wide])
        cross(c).start()
    mine = nrm[pl.ds(pl.multiple_of(core * half, half), half), :]
    for c in range(chunks):
        own = dot1(mine, w_ref[:, c * wide : (c + 1) * wide])
        cross(c).wait_recv()
        out_ref[:, c * wide : (c + 1) * wide] = (own + other[c]).astype(BF16)
    for c in range(chunks):
        cross(c).wait_send()

    @pl.when(me < n - 1)
    def _():
        for h in range(heads):
            for u in range(UNITS):
                hop(h, u).wait_send()


def shards(queries, key_rows, value_rows, strengths, log_gate, keep_flag, norm_gain, out_weight):
    tok = queries.shape[0]
    heads = strengths.shape[0]
    keys2 = key_rows.reshape(tok, -1)
    vals2 = value_rows.reshape(tok, -1)
    vmem = pl.BlockSpec(memory_space=pltpu.VMEM)
    hbm = pl.BlockSpec(memory_space=pltpu.HBM)
    wide = out_weight.shape[1]
    return pl.pallas_call(
        functools.partial(chain_kernel, heads),
        out_shape=jax.ShapeDtypeStruct((tok // 2, wide), BF16),
        in_specs=[hbm, vmem, vmem, hbm, hbm, hbm, hbm, hbm],
        out_specs=vmem,
        scratch_shapes=[
            pltpu.VMEM((heads, 2 * tok, 2 * tok), F32),
            pltpu.VMEM((heads, 2 * tok, 2 * tok), BF16),
            pltpu.VMEM((heads, 2 * tok, 2 * tok), BF16),
            pltpu.VMEM((4 * heads, tok), F32),
            pltpu.VMEM(queries.shape, BF16),
            pltpu.VMEM(strengths.shape, F32),
            pltpu.VMEM(log_gate.shape, F32),
            pltpu.VMEM((1, tok), jnp.int32),
            pltpu.VMEM((1, heads * DV), F32),
            pltpu.VMEM(out_weight.shape, BF16),
            pltpu.SemaphoreType.DMA((6,)),
            pltpu.VMEM((heads, DV, DK), F32),
            pltpu.VMEM((heads, tok, DK + DV), F32),
            pltpu.VMEM((heads, DV, DK), F32),
            pltpu.VMEM((heads, DV, DK), F32),
            pltpu.VMEM((heads, DK, DK), BF16),
            pltpu.VMEM((heads, DK, DK), BF16),
            pltpu.VMEM((tok, heads * DV), BF16),
            pltpu.VMEM((CHUNKS, tok // 2, wide // CHUNKS), F32),
            pltpu.VMEM((CHUNKS, tok // 2, wide // CHUNKS), F32),
            pltpu.SemaphoreType.DMA((heads * UNITS,)),
            pltpu.SemaphoreType.DMA((heads * UNITS,)),
            pltpu.SemaphoreType.DMA((CHUNKS,)),
            pltpu.SemaphoreType.DMA((CHUNKS,)),
        ],
        compiler_params=pltpu.CompilerParams(vmem_limit_bytes=62 << 20, collective_id=0, has_side_effects=True),
        name="chain_project",
    )(queries, keys2, vals2, strengths, log_gate, keep_flag[None, :], norm_gain[None, :], out_weight)


def solution(mesh):
    in_specs = (
        P(("groups", "seq"), "head"),
        P(("groups", "seq"), None, "head"),
        P(("groups", "seq"), None, "head"),
        P("head", None, ("groups", "seq")),
        P("head", ("groups", "seq")),
        P(("groups", "seq")),
        P("head"),
        P("head", None),
    )
    out_specs = P(("groups", "seq", "head"), None)
    return jax.shard_map(shards, mesh=mesh, in_specs=in_specs, out_specs=out_specs, check_vma=False)
```

```python
import functools

import jax
import jax.numpy as jnp
from jax import lax
from jax.experimental import pallas as pl
from jax.experimental.pallas import tpu as pltpu
from jax.sharding import PartitionSpec as P

DK = 128
DV = 128
UNITS = 4
CHUNKS = 4
F32 = jnp.float32
BF16 = jnp.bfloat16


def split2(x):
    hi = x.astype(BF16)
    return hi, (x - hi.astype(F32)).astype(BF16)


def dot1(a, b):
    return jnp.dot(a, b, preferred_element_type=F32)


def mm3(a, b):
    return dot1(a[0], b[0]) + (dot1(a[0], b[1]) + dot1(a[1], b[0]))


def dot_nt(a, b):
    return lax.dot_general(a, b, (((1,), (1,)), ((), ())), preferred_element_type=F32)


def local_maps(
    heads, loads, k_ref, v_ref, bias_ref, th_sc, tl_sc, reads_ref,
    a_sc, xh_sc, xl_sc, small_ref, q_ref, str_ref, log_ref, keep_ref,
):
    tok = q_ref.shape[0]
    for load in loads[:3]:
        load.wait()
    live = keep_ref[...].astype(F32)
    small_ref[...] = jnp.zeros_like(small_ref)
    small_ref[:heads] = str_ref[:, 0, :] * live
    small_ref[heads : 2 * heads] = str_ref[:, 1, :] * live
    small_ref[2 * heads : 3 * heads] = log_ref[...] * live
    size = 2 * tok
    width = heads * DK
    row_t = lax.broadcasted_iota(jnp.int32, (tok, tok), 0)
    col_t = lax.broadcasted_iota(jnp.int32, (tok, tok), 1)
    incl = row_t >= col_t
    strict = row_t > col_t
    small = small_ref[...]
    s1 = small.astype(BF16)
    rest = small - s1.astype(F32)
    s2 = rest.astype(BF16)
    s3 = (rest - s2.astype(F32)).astype(BF16)
    upper = jnp.where(row_t <= col_t, 1.0, 0.0).astype(BF16)
    cum = dot1(s1, upper) + (dot1(s2, upper) + dot1(s3, upper))
    srows = small.shape[0]
    cols = jnp.concatenate([small, cum, jnp.zeros((tok - 2 * srows, tok), F32)], axis=0).T

    row_i = lax.broadcasted_iota(jnp.int32, (size, size), 0)
    col_i = lax.broadcasted_iota(jnp.int32, (size, size), 1)
    time_r = jnp.where(row_i < tok, 2 * row_i, 2 * row_i - 2 * tok + 1)
    time_c = jnp.where(col_i < tok, 2 * col_i, 2 * col_i - 2 * tok + 1)

    for h in range(heads):
        kk = [k_ref[:, j * width + h * DK : j * width + (h + 1) * DK] for j in range(2)]
        keys = jnp.concatenate(kk, axis=0)
        gram = dot_nt(keys, keys)
        cum_col = cols[:, srows + 2 * heads + h : srows + 2 * heads + h + 1]
        cum_row = cum[2 * heads + h : 2 * heads + h + 1, :]
        decay = jnp.where(incl, jnp.exp(jnp.where(incl, cum_col - cum_row, 0.0)), 0.0)
        decay_s = jnp.where(strict, decay, 0.0)
        kf = keys.astype(F32)
        r2 = 1.0 / (jnp.sum(kf * kf, axis=-1, keepdims=True) + 1e-06)
        beta = jnp.concatenate([cols[:, h : h + 1], cols[:, heads + h : heads + h + 1]], axis=0)
        factor = jnp.concatenate(
            [jnp.concatenate([decay_s, decay_s], axis=1), jnp.concatenate([decay, decay_s], axis=1)], axis=0
        )
        a_full = (beta * r2) * factor * gram
        a_sc[h] = a_full
        first = jnp.where((time_r ^ time_c) == 1, a_full, 0.0)
        x0 = jnp.where(time_r == time_c, 1.0, 0.0) - first
        xh_sc[h], xl_sc[h] = split2(x0)

    bit = 1
    while 2 << bit <= size:
        low = time_c >> bit
        picked = ((time_r >> bit) == (low | 1)) & ((low & 1) == 0)
        for h in range(heads):
            b = split2(jnp.where(picked, a_sc[h], 0.0))
            x = (xh_sc[h], xl_sc[h])
            y = split2(mm3(b, x))
            d = split2(mm3(x, y))
            xh_sc[h] = x[0] - d[0]
            xl_sc[h] = x[1] - d[1]
        bit += 1

    loads[3].wait()
    for h in range(heads):
        kk = [k_ref[:, j * width + h * DK : j * width + (h + 1) * DK] for j in range(2)]
        vv = [v_ref[:, j * width + h * DV : j * width + (h + 1) * DV] for j in range(2)]
        keys = jnp.concatenate(kk, axis=0)
        vals = jnp.concatenate(vv, axis=0).astype(F32)
        kf = keys.astype(F32)
        ss = jnp.sum(kf * kf, axis=-1, keepdims=True) + 1e-06
        beta = jnp.concatenate([cols[:, h : h + 1], cols[:, heads + h : heads + h + 1]], axis=0)
        cum_col = cols[:, srows + 2 * heads + h : srows + 2 * heads + h + 1]
        cum_row = cum[2 * heads + h : 2 * heads + h + 1, :]
        ecum = jnp.exp(cum_col)
        ecum2 = jnp.concatenate([ecum, ecum], axis=0)
        rhs = jnp.concatenate([(beta * ecum2 / ss) * kf, (beta * lax.rsqrt(ss)) * vals], axis=1)
        wu = mm3((xh_sc[h], xl_sc[h]), split2(rhs))
        q = q_ref[:, h * DK : (h + 1) * DK]
        qf = q.astype(F32)
        rq = lax.rsqrt(jnp.sum(qf * qf, axis=-1, keepdims=True) + 1e-06)
        decay = jnp.where(incl, jnp.exp(jnp.where(incl, cum_col - cum_row, 0.0)), 0.0)
        qmix = jnp.concatenate([decay, decay], axis=1) * (rq * dot_nt(q, keys))
        last = cum_row[:, tok - 1 : tok]
        to_end = jnp.exp(last - cum_row)
        kt = kf.T * jnp.concatenate([to_end, to_end], axis=1)
        both = mm3(split2(jnp.concatenate([qmix, kt], axis=0)), split2(wu))
        reads_ref[h, :, :DK] = (ecum * rq) * qf - both[:tok, :DK]
        reads_ref[h, :, DK:] = both[:tok, DK:]
        elast = jnp.exp(last)
        th_sc[h], tl_sc[h] = split2(jnp.where(row_t == col_t, elast, 0.0) - both[tok:, :DK].T)
        bias_ref[h] = both[tok:, DK:].T


def chain_kernel(
    heads, q_hbm, k_hbm, v_hbm, str_hbm, log_hbm, keep_hbm, gain_hbm, w_hbm, out_ref,
    k_raw, v_raw, k_ref, v_ref,
    a_sc, xh_sc, xl_sc, small_ref, q_ref, str_ref, log_ref, keep_ref,
    gain_ref, w_ref, load_sem, bias_ref, reads_ref, sin, sout, th_sc, tl_sc, nrm, part, other, send_sem, recv_sem, xsend, xrecv,
):
    pairs = (
        (str_hbm, str_ref),
        (log_hbm, log_ref),
        (keep_hbm, keep_ref),
        (q_hbm, q_ref),
        (gain_hbm, gain_ref),
        (w_hbm, w_ref),
        (k_hbm, k_raw),
        (v_hbm, v_raw),
    )
    loads = [pltpu.make_async_copy(a, b, load_sem.at[i]) for i, (a, b) in enumerate(pairs)]
    for load in loads:
        load.start()
    n = lax.axis_size("seq")
    me = lax.axis_index("seq")
    core = lax.axis_index("head")
    sibling = 1 - core
    right = lax.rem(me + 1, n)
    barrier = pltpu.get_barrier_semaphore()

    def signal(where):
        pl.semaphore_signal(barrier, inc=1, device_id=where, device_id_type=pl.DeviceIdType.MESH)

    signal({"head": sibling})

    @pl.when(me < n - 1)
    def _():
        signal({"seq": right})

    @pl.when(me > 0)
    def _():
        signal({"seq": lax.rem(me + n - 1, n)})

    for load, raw, flat in ((loads[6], k_raw, k_ref), (loads[7], v_raw, v_ref)):
        load.wait()
        flat[...] = raw[...].reshape(flat.shape)
    local_maps(
        heads, loads, k_ref, v_ref, bias_ref, th_sc, tl_sc, reads_ref,
        a_sc, xh_sc, xl_sc, small_ref, q_ref, str_ref, log_ref, keep_ref,
    )
    inner = (me > 0) & (me < n - 1)

    @pl.when(inner)
    def _():
        pl.semaphore_wait(barrier, 3)

    @pl.when(jnp.logical_not(inner))
    def _():
        pl.semaphore_wait(barrier, 2)

    rows = DV // UNITS

    def hop(h, u):
        span = pl.ds(u * rows, rows)
        return pltpu.make_async_remote_copy(
            src_ref=sout.at[h, span],
            dst_ref=sin.at[h, span],
            send_sem=send_sem.at[h * UNITS + u],
            recv_sem=recv_sem.at[h * UNITS + u],
            device_id={"seq": right},
            device_id_type=pl.DeviceIdType.MESH,
        )

    def read(h):
        state = split2(sin[h])
        reach = split2(reads_ref[h, :, :DK])
        seen = dot_nt(reach[0], state[0]) + (dot_nt(reach[0], state[1]) + dot_nt(reach[1], state[0]))
        att = reads_ref[h, :, DK:] + seen
        inv = lax.rsqrt(jnp.mean(att * att, axis=-1, keepdims=True) + 1e-05)
        nrm[:, h * DV : (h + 1) * DV] = (att * inv * gain_ref[:, h * DV : (h + 1) * DV]).astype(BF16)

    loads[4].wait()
    for h in range(heads):
        for u in range(UNITS):
            lo, hi = u * rows, (u + 1) * rows

            @pl.when(me == 0)
            def _():
                sin[h, lo:hi] = jnp.zeros((rows, DK), F32)
                sout[h, lo:hi] = bias_ref[h, lo:hi]

            @pl.when(me > 0)
            def _():
                hop(h, u).wait_recv()

            @pl.when(inner)
            def _():
                moved = mm3(split2(sin[h, lo:hi]), (th_sc[h], tl_sc[h]))
                sout[h, lo:hi] = moved + bias_ref[h, lo:hi]

            @pl.when(me < n - 1)
            def _():
                hop(h, u).start()

        @pl.when(me == n - 1)
        def _():
            read(h)

    @pl.when(me < n - 1)
    def _():
        for h in range(heads):
            read(h)

    loads[5].wait()
    half = nrm.shape[0] // 2
    wide = part.shape[-1]
    chunks = part.shape[0]

    def cross(c):
        return pltpu.make_async_remote_copy(
            src_ref=part.at[c],
            dst_ref=other.at[c],
            send_sem=xsend.at[c],
            recv_sem=xrecv.at[c],
            device_id={"head": sibling},
            device_id_type=pl.DeviceIdType.MESH,
        )

    theirs = nrm[pl.ds(pl.multiple_of(sibling * half, half), half), :]
    for c in range(chunks):
        part[c] = dot1(theirs, w_ref[:, c * wide : (c + 1) * wide])
        cross(c).start()
    mine = nrm[pl.ds(pl.multiple_of(core * half, half), half), :]
    for c in range(chunks):
        own = dot1(mine, w_ref[:, c * wide : (c + 1) * wide])
        cross(c).wait_recv()
        out_ref[:, c * wide : (c + 1) * wide] = (own + other[c]).astype(BF16)
    for c in range(chunks):
        cross(c).wait_send()

    @pl.when(me < n - 1)
    def _():
        for h in range(heads):
            for u in range(UNITS):
                hop(h, u).wait_send()


def shards(queries, key_rows, value_rows, strengths, log_gate, keep_flag, norm_gain, out_weight):
    tok = queries.shape[0]
    heads = strengths.shape[0]
    vmem = pl.BlockSpec(memory_space=pltpu.VMEM)
    hbm = pl.BlockSpec(memory_space=pltpu.HBM)
    wide = out_weight.shape[1]
    return pl.pallas_call(
        functools.partial(chain_kernel, heads),
        out_shape=jax.ShapeDtypeStruct((tok // 2, wide), BF16),
        in_specs=[hbm] * 8,
        out_specs=vmem,
        scratch_shapes=[
            pltpu.VMEM(key_rows.shape, BF16),
            pltpu.VMEM(value_rows.shape, BF16),
            pltpu.VMEM((tok, 2 * heads * DK), BF16),
            pltpu.VMEM((tok, 2 * heads * DV), BF16),
            pltpu.VMEM((heads, 2 * tok, 2 * tok), F32),
            pltpu.VMEM((heads, 2 * tok, 2 * tok), BF16),
            pltpu.VMEM((heads, 2 * tok, 2 * tok), BF16),
            pltpu.VMEM((4 * heads, tok), F32),
            pltpu.VMEM(queries.shape, BF16),
            pltpu.VMEM(strengths.shape, F32),
            pltpu.VMEM(log_gate.shape, F32),
            pltpu.VMEM((1, tok), jnp.int32),
            pltpu.VMEM((1, heads * DV), F32),
            pltpu.VMEM(out_weight.shape, BF16),
            pltpu.SemaphoreType.DMA((8,)),
            pltpu.VMEM((heads, DV, DK), F32),
            pltpu.VMEM((heads, tok, DK + DV), F32),
            pltpu.VMEM((heads, DV, DK), F32),
            pltpu.VMEM((heads, DV, DK), F32),
            pltpu.VMEM((heads, DK, DK), BF16),
            pltpu.VMEM((heads, DK, DK), BF16),
            pltpu.VMEM((tok, heads * DV), BF16),
            pltpu.VMEM((CHUNKS, tok // 2, wide // CHUNKS), F32),
            pltpu.VMEM((CHUNKS, tok // 2, wide // CHUNKS), F32),
            pltpu.SemaphoreType.DMA((heads * UNITS,)),
            pltpu.SemaphoreType.DMA((heads * UNITS,)),
            pltpu.SemaphoreType.DMA((CHUNKS,)),
            pltpu.SemaphoreType.DMA((CHUNKS,)),
        ],
        compiler_params=pltpu.CompilerParams(vmem_limit_bytes=62 << 20, collective_id=0, has_side_effects=True),
        name="chain_project",
    )(queries, key_rows, value_rows, strengths, log_gate, keep_flag[None, :], norm_gain[None, :], out_weight)


def solution(mesh):
    in_specs = (
        P(("groups", "seq"), "head"),
        P(("groups", "seq"), None, "head"),
        P(("groups", "seq"), None, "head"),
        P("head", None, ("groups", "seq")),
        P("head", ("groups", "seq")),
        P(("groups", "seq")),
        P("head"),
        P("head", None),
    )
    out_specs = P(("groups", "seq", "head"), None)
    return jax.shard_map(shards, mesh=mesh, in_specs=in_specs, out_specs=out_specs, check_vma=False)
```
